32 devices in a mesh: row: 4 (over y, core), col: 8 (over z, x).
Axes of the slice: x: 2, y: 2, z: 4, core: 2. Of those that a mesh axis runs over, the one named last changes fastest.
Arguments:
- records: bfloat16 [16, 8192, 4096], P('col', 'row'), may hold values from -6 to 6
- centre_bins: int32 [2], replicated, may hold values from 33 to 2016, as said below
- segment_valid: int32 [16], replicated, may hold values 0 or 1
Outputs:
- coherency: float32 [2, 2, 8192, 8192], P(None, None, 'row', 'col')
The draws below stay inside these ranges and needn't reach their ends.
Inputs may be any that keep to these rules, and one draw needn't show every extreme that they name: `centre_bins`: the selected bins are all different and one of them is the highest allowed; their bands may intersect.
All inputs are finite; a program needn't handle non-finite values.
Results may differ from the reference program's by a relative error of at most 0.0049.
Values may be sent and summed in bfloat16 or wider, within the bound.
No kernel may reach another device: no remote copies, remote signals or barrier semaphores. Data moves between devices by JAX's collectives and lax.ppermute only.
A program may use at most 256 MiB of HBM per device.

```python
import math
import jax
import jax.numpy as jnp
from jax import lax

C = 8192
L = 4096
BAND = 64
NSEL = 2
S = 16


def draw_centre_bins(key, part):
    lowest = BAND // 2 + 1
    highest = L // 2 - BAND // 2
    span = highest - lowest
    first_key = jax.random.fold_in(key, 11)
    step_key = jax.random.fold_in(key, 12)
    place_key = jax.random.fold_in(key, 13)
    first = jax.random.randint(first_key, (), 0, span, dtype=jnp.int32)
    step = jax.random.randint(step_key, (), 1, span, dtype=jnp.int32)
    counter = jnp.arange(NSEL, dtype=jnp.int32)
    others = lowest + (first + counter * step) % span
    values = jnp.where(counter == 0, highest, others).astype(jnp.int32)
    shift_value = jax.random.randint(place_key, (), 0, NSEL, dtype=jnp.int32)
    return jnp.roll(values, shift_value).astype(jnp.int32)


def place_ends(entries, key, least, high):
    spot = [jax.random.randint(jax.random.fold_in(key, axis), (), 0, length) for axis, length in enumerate(entries.shape)]
    widest = entries.shape.index(max(entries.shape))
    beside = spot[:widest] + [(spot[widest] + 1) % entries.shape[widest]] + spot[widest + 1:]
    return entries.at[tuple(spot)].set(least).at[tuple(beside)].set(high)


def steps_of(rng, dims, shards, least, top_value):
    def one(position, parts):
        draws = jax.random.uniform(jax.random.fold_in(jax.random.fold_in(rng, 6), position), (parts,), jnp.float32, least / len(shards), top_value / len(shards))
        return jnp.repeat(jnp.exp(draws), dims[position] // parts).reshape((-1,) + (1,) * (len(dims) - position - 1))

    loudness = one(*shards[0])
    for cut in shards[1:]:
        loudness = loudness * one(*cut)
    return loudness


def noise(stream_key, shape, deviation, reach, pieces=(), held_as=jnp.bfloat16):
    result = deviation * jax.random.normal(stream_key, shape, jnp.float32)
    if pieces:
        result = result * steps_of(stream_key, shape, pieces, -0.22, 0.18)
    return jnp.clip(result, -reach, reach).astype(held_as)


def setup_inputs(seed: int = 0) -> dict:
    seeds = jax.random.split(jax.random.key(seed), 4)
    records = noise(seeds[0], (S, C, L), 1.0, 6.0, ((0, 8), (1, 4)))
    centre_bins = draw_centre_bins(jax.random.fold_in(seeds[3], 71), 0)
    segment_valid = place_ends((jax.random.randint(seeds[2], (S,), 0, 3) < 2).astype(jnp.int32), jax.random.fold_in(seeds[2], 1), 0, 1)
    return dict(records=records, centre_bins=centre_bins, segment_valid=segment_valid)


def transform_table(centre_bins, length):
    samples = lax.broadcasted_iota(jnp.int32, (length, 1, 1), 0)
    offsets = jnp.arange(BAND, dtype=jnp.int32) - BAND // 2
    frequencies = centre_bins.astype(jnp.int32)[:, None] + offsets[None, :]
    phases = samples * frequencies[None, :, :] % length
    angles = phases.astype(jnp.float32) * (2.0 * math.pi / length)
    factor = 1.0 / math.sqrt(length)
    stacked = jnp.stack([jnp.cos(angles) * factor, -jnp.sin(angles) * factor], axis=2)
    return stacked.reshape(length, NSEL * 2 * BAND).astype(jnp.bfloat16)

def whiten(spectra):
    grouped = spectra.reshape(spectra.shape[0], NSEL, 2, BAND)
    real_part = grouped[:, :, 0, :]
    imag_part = grouped[:, :, 1, :]
    amplitude = lax.optimization_barrier(jnp.mean(jnp.sqrt(real_part * real_part + imag_part * imag_part), axis=2))
    scaled = grouped / (amplitude[:, :, None, None] + 1e-06)
    return scaled.reshape(spectra.shape[0], NSEL * 2 * BAND).astype(jnp.bfloat16)

def reference(records, centre_bins, segment_valid):
    weights = transform_table(centre_bins, L)
    spectra = jnp.dot(records.reshape(S * C, L), weights, preferred_element_type=jnp.float32)
    whitened = whiten(spectra).reshape(S, C, NSEL * 2 * BAND)
    valid_weight = segment_valid.astype(jnp.bfloat16)
    outputs = []
    for band_index in range(NSEL):
        bin_block = whitened[:, :, band_index * 2 * BAND:(band_index + 1) * 2 * BAND]
        turned = jnp.concatenate([-bin_block[:, :, BAND:], bin_block[:, :, :BAND]], axis=2)
        left_side = jnp.transpose(bin_block * valid_weight[:, None, None], (1, 0, 2)).reshape(C, S * 2 * BAND)
        right_real = jnp.transpose(bin_block, (1, 0, 2)).reshape(C, S * 2 * BAND)
        right_imag = jnp.transpose(turned, (1, 0, 2)).reshape(C, S * 2 * BAND)
        real_tile = jnp.dot(left_side, right_real.T, preferred_element_type=jnp.float32)
        imag_tile = jnp.dot(left_side, right_imag.T, preferred_element_type=jnp.float32)
        outputs.append(jnp.stack([real_tile, imag_tile], axis=0))
    return jnp.stack(outputs, axis=0) * (1.0 / (S * BAND))
```

```python
import functools
import math

import jax
import jax.numpy as jnp
from jax import lax
from jax.experimental import pallas as pl
from jax.experimental.pallas import tpu as pltpu
from jax.sharding import PartitionSpec as P


BAND = 64
NSEL = 2
LANES = 2 * BAND
FINE = 64


def fill_table(length, centre_ref, table_ref):
    lane = lax.broadcasted_iota(jnp.int32, (FINE, LANES), 1)
    step = lax.broadcasted_iota(jnp.int32, (FINE, LANES), 0)
    centre = jnp.where(lane < BAND, centre_ref[0], centre_ref[1])
    frequency = centre - BAND // 2 + jnp.where(lane < BAND, lane, lane - BAND)
    scale = 2.0 * math.pi / length
    factor = 1.0 / math.sqrt(length)
    fine = lax.rem(step * frequency, length).astype(jnp.float32) * scale
    fine_cos, fine_sin = jnp.cos(fine), jnp.sin(fine)
    for first in range(0, length // FINE, FINE):
        many = min(FINE, length // FINE - first)
        coarse = lax.rem((step + first) * frequency * FINE, length).astype(jnp.float32) * scale
        coarse_cos, coarse_sin = jnp.cos(coarse) * factor, jnp.sin(coarse) * factor
        for index in range(many):
            c = coarse_cos[index : index + 1, :]
            s = coarse_sin[index : index + 1, :]
            real = c * fine_cos - s * fine_sin
            imag = -(s * fine_cos + c * fine_sin)
            rows = pl.ds((first + index) * FINE, FINE)
            table_ref[rows, :LANES] = real.astype(jnp.bfloat16)
            table_ref[rows, LANES:] = imag.astype(jnp.bfloat16)


def front_kernel(place_ref, valid_ref, centre_ref, records_ref, out_ref, table_ref):
    segments, rows, length = records_ref.shape

    @pl.when(pl.program_id(0) == 0)
    def _():
        fill_table(length, centre_ref, table_ref)

    spectra = jnp.dot(
        records_ref[...].reshape(segments * rows, length), table_ref[...], preferred_element_type=jnp.float32
    )
    real, imag = spectra[:, :LANES], spectra[:, LANES:]
    size = jnp.sqrt(real * real + imag * imag)
    left = lax.broadcasted_iota(jnp.int32, (LANES, LANES), 0) < BAND
    top = lax.broadcasted_iota(jnp.int32, (LANES, LANES), 1) < BAND
    same = (left == top).astype(jnp.bfloat16)
    total = jnp.zeros_like(size)
    rest = size
    for _ in range(3):
        piece = rest.astype(jnp.bfloat16)
        total = total + jnp.dot(piece, same, preferred_element_type=jnp.float32)
        rest = rest - piece.astype(jnp.float32)
    inverse = 1.0 / (total * (1.0 / BAND) + 1e-06)
    lane = lax.broadcasted_iota(jnp.int32, (rows, LANES), 1) < BAND
    keep = [valid_ref[place_ref[2] * segments + s].astype(jnp.float32) for s in range(segments)]
    for part, values in ((0, real), (1, imag)):
        scaled = values * inverse
        first = scaled[:rows] * keep[0]
        second = scaled[rows:] * keep[1]
        here = pl.ds(part * LANES, LANES)
        out_ref[0, :, here] = jnp.where(lane, first, pltpu.roll(second, BAND, 1)).astype(jnp.bfloat16)
        out_ref[1, :, here] = jnp.where(lane, pltpu.roll(first, BAND, 1), second).astype(jnp.bfloat16)


def front(place, far, valid, centres, records, half_rows):
    segments, _, length = records.shape
    tile = 256
    tiles = half_rows // tile
    half = lambda s: 1 - s[0] if far else s[0]
    return pl.pallas_call(
        front_kernel,
        out_shape=jax.ShapeDtypeStruct((NSEL, half_rows, 2 * LANES), jnp.bfloat16),
        grid_spec=pltpu.PrefetchScalarGridSpec(
            num_scalar_prefetch=3,
            grid=(tiles,),
            in_specs=[pl.BlockSpec((segments, tile, length), lambda i, s, v, c: (0, half(s) * tiles + i, 0))],
            out_specs=pl.BlockSpec((NSEL, tile, 2 * LANES), lambda i, s, v, c: (0, i, 0)),
            scratch_shapes=[pltpu.VMEM((length, 2 * LANES), jnp.bfloat16)],
        ),
        cost_estimate=pl.CostEstimate(
            flops=2 * segments * half_rows * length * 256,
            bytes_accessed=2 * segments * half_rows * length,
            transcendentals=0,
        ),
    )(place, valid, centres, records)


def back_kernel(factor, units, partial, scalar_ref, *refs):
    row_refs = refs[:units]
    col_refs = [refs[units + 4 * u : units + 4 * u + 4] for u in range(units)]
    partial_ref = refs[5 * units] if partial else None
    out_ref, right_ref, arrived = refs[-3:]
    band = pl.program_id(0)

    def copies(which, at):
        return [
            pltpu.make_async_copy(col_refs[u][which].at[at], right_ref.at[at, u], arrived.at[at, u])
            for u in range(units)
        ]

    @pl.when((band == 0) & (pl.program_id(1) == 0))
    def _():
        for which in range(4):

            @pl.when(scalar_ref[1] == which)
            def _():
                for at in range(NSEL):
                    for copy in copies(which, at):
                        copy.start()

    for at in range(NSEL):

        @pl.when((band == at) & (pl.program_id(1) == 0))
        def _():
            for copy in copies(0, at):
                copy.wait()

    rows = [r[0] for r in row_refs]
    real = jnp.concatenate(rows, axis=1)
    turned = jnp.concatenate([p for r in rows for p in (r[:, LANES:], -r[:, :LANES])], axis=1)
    left = jnp.concatenate([real, turned], axis=0)
    right = jnp.concatenate([right_ref[band, u] for u in range(units)], axis=1)
    product = lax.dot_general(left, right, (((1,), (1,)), ((), ())), preferred_element_type=jnp.float32)
    many = real.shape[0]
    for part in range(2):
        value = product[part * many : (part + 1) * many] * factor
        if partial:
            value = value + partial_ref[0, part].astype(jnp.float32)
        out_ref[0, part] = value.astype(out_ref.dtype)


def back(place, far, start, count, row_units, col_units, factor, partial=None, held=None, row_count=None):
    units, col_count = len(row_units), col_units[0][0].shape[1]
    half_rows = col_count
    tile = math.gcd(count, 512)
    tiles = count // tile
    final = row_count is not None
    half = lambda s: 1 - s[0] if far else s[0]
    kept = pl.BlockSpec(memory_space=pltpu.HBM)
    in_specs = [
        pl.BlockSpec((1, tile, 2 * LANES), lambda b, i, s, first=first: (b, first // tile + i, 0))
        for _, first in row_units
    ]
    in_specs += [kept] * (4 * units)
    operands = [place, *(x for x, _ in row_units), *(c for col in col_units for c in col)]
    out_spec = pl.BlockSpec((1, 2, tile, col_count), lambda b, i, s: (b, 0, i, 0))
    if final:
        out_spec = pl.BlockSpec(
            (1, 2, tile, col_count), lambda b, i, s: (b, 0, (half(s) * half_rows + start) // tile + i, 0)
        )
    if partial is not None:
        operands.append(partial)
        begin = start // tile if final else 0
        in_specs.append(pl.BlockSpec((1, 2, tile, col_count), lambda b, i, s: (b, 0, begin + i, 0)))
    aliases = {}
    if held is not None:
        aliases = {len(operands): 0}
        operands.append(held)
        in_specs.append(kept)
    shape = (NSEL, 2, row_count if final else count, col_count)
    return pl.pallas_call(
        functools.partial(back_kernel, factor, units, partial is not None),
        out_shape=jax.ShapeDtypeStruct(shape, jnp.float32 if final else jnp.bfloat16),
        grid_spec=pltpu.PrefetchScalarGridSpec(
            num_scalar_prefetch=1,
            grid=(NSEL, tiles),
            in_specs=in_specs,
            out_specs=out_spec,
            scratch_shapes=[
                pltpu.VMEM((NSEL, units, col_count, 2 * LANES), jnp.bfloat16),
                pltpu.SemaphoreType.DMA((NSEL, units)),
            ],
        ),
        input_output_aliases=aliases,
        cost_estimate=pl.CostEstimate(
            flops=2 * NSEL * 2 * count * col_count * 256 * units,
            bytes_accessed=(4 if final else 2) * NSEL * 2 * count * col_count,
            transcendentals=0,
        ),
    )(*operands)


def ring_shards(records, centre_bins, segment_valid):
    _, row_count, _ = records.shape
    col_size = lax.axis_size("col")
    half_rows = row_count // 2
    row_index, col_index = lax.axis_index("row"), lax.axis_index("col")
    factor = 1.0 / (segment_valid.shape[0] * BAND)

    around = [(c, (c + 2) % col_size) for c in range(col_size)]
    across = [(c, c ^ 1) for c in range(col_size)]
    flat = lambda r, c: r * col_size + c
    holders = [(c // 2, c) for c in range(col_size)]
    to_y = [(flat(r, c), flat(r ^ 2, c)) for r, c in holders]
    to_core = [(flat(r, c), flat(r ^ 1, c)) for r, c in holders]
    to_far_core = [(flat(r ^ 2, c), flat(r ^ 3, c)) for r, c in holders]

    def ring(x):
        return lax.ppermute(x, "col", around)

    def cross(x):
        return lax.ppermute(x, "col", across)

    def column(x):
        over = lax.ppermute(x, ("row", "col"), to_y)
        left = lax.ppermute(x, ("row", "col"), to_core)
        right = lax.ppermute(over, ("row", "col"), to_far_core)
        return [x, left, over, right]

    apart = row_index ^ (col_index // 2)
    place = jnp.stack([col_index % 2, apart, col_index]).astype(jnp.int32)
    far = front(place, True, segment_valid, centre_bins, records, half_rows)
    near = front(place, False, segment_valid, centre_bins, records, half_rows)

    z1f = ring(far)
    x0n = cross(far)
    z1n = ring(near)
    x0f = cross(near)
    z2f = ring(z1f)
    x1n = cross(z1f)
    x1f = cross(z1n)
    z3f = ring(z2f)
    z2n = ring(z1n)
    x2n = cross(z2f)
    x2f = cross(z2n)
    z3n = ring(z2n)
    x3n = cross(z3f)
    x3f = cross(z3n)

    near_units = dict(o=near, a=x0n, b=z1n, c=x1n, d=z2n, e=x2n, g=z3n, h=x3n)
    far_units = dict(o=far, a=x0f, b=z1f, c=x1f, d=z2f, e=x2f, g=z3f, h=x3f)
    columns = {u: column(x) for u, x in near_units.items()}

    def add(name, units, partial=None, held=None, final=None):
        far_rows = name[-1] == "f"
        row_units = [((far_units if far_rows else near_units)[u], 0) for u in units]
        col_units = [columns[u] for u in units]
        return back(place, far_rows, 0, half_rows, row_units, col_units, factor, partial, held, final)

    part_n = add("pre1n", "oa")
    part_f = add("pre1f", "oa")
    part_n = add("pre2n", "bc", part_n)
    part_f = add("pre2f", "bc", part_f)
    part_n = add("pre3n", "de", part_n)
    out = add("finn", "gh", part_n, None, row_count)
    out = add("finf", "degh", part_f, out, row_count)
    return out


def gather_shards(records, centre_bins, segment_valid):
    seg_count, row_count, length = records.shape
    samples = lax.broadcasted_iota(jnp.int32, (length, 1, 1), 0)
    offsets = jnp.arange(BAND, dtype=jnp.int32) - BAND // 2
    frequencies = centre_bins[:, None] + offsets[None, :]
    angles = (samples * frequencies[None, :, :] % length).astype(jnp.float32) * (2.0 * math.pi / length)
    scale = 1.0 / math.sqrt(length)
    table = jnp.stack([jnp.cos(angles) * scale, -jnp.sin(angles) * scale], axis=2)
    table = table.reshape(length, NSEL * LANES).astype(jnp.bfloat16)
    spectra = jnp.dot(
        records.reshape(seg_count * row_count, length), table, preferred_element_type=jnp.float32
    ).reshape(seg_count * row_count, NSEL, 2, BAND)
    amplitude = jnp.mean(jnp.sqrt(spectra[:, :, 0] ** 2 + spectra[:, :, 1] ** 2), axis=2)
    whitened = (spectra / (amplitude[:, :, None, None] + 1e-06)).astype(jnp.bfloat16)
    row_side = lax.all_gather(whitened.reshape(seg_count, row_count, NSEL * LANES), "col", axis=0, tiled=True)
    row_size, col_size = lax.axis_size("row"), lax.axis_size("col")
    col_count = row_count * row_size // col_size
    column_index = lax.axis_index("col")
    start = column_index * col_count
    local = lax.dynamic_slice_in_dim(row_side, start % row_count, col_count, 1)
    local = jnp.where(lax.axis_index("row") == start // row_count, local, jnp.zeros_like(local))
    col_side = lax.psum(local, "row")
    row_side = row_side * segment_valid.astype(jnp.bfloat16)[:, None, None]
    results = []
    for band in range(NSEL):
        left = row_side[:, :, band * LANES : (band + 1) * LANES]
        right = col_side[:, :, band * LANES : (band + 1) * LANES]
        turned = jnp.concatenate([-right[:, :, BAND:], right[:, :, :BAND]], axis=2)
        for side in (right, turned):
            results.append(
                lax.dot_general(left, side, (((0, 2), (0, 2)), ((), ())), preferred_element_type=jnp.float32)
            )
    total = jnp.stack(results).reshape(NSEL, 2, row_count, col_count)
    return total * (1.0 / (segment_valid.shape[0] * BAND))


def solution(mesh):
    placed = (P("col", "row", None), P(), P())
    out = P(None, None, "row", "col")
    on_ring = mesh.shape["col"] == 2 * mesh.shape["row"] and mesh.shape["row"] == 4
    shards = ring_shards if on_ring else gather_shards
    return jax.shard_map(shards, mesh=mesh, in_specs=placed, out_specs=out, check_vma=False)
```
